32 devices in a mesh: row: 4 (over x, core), col: 8 (over z, y).
Axes of the slice: x: 2, y: 2, z: 4, core: 2. Of those that a mesh axis runs over, the one named last changes fastest.
Arguments:
- eigenvectors: float32 [2048, 1024], P('row', 'col'), may hold values from -6 to 6
- householder: float32 [3, 8, 512, 256], P(None, 'row', None, 'col'), may hold values from -6 to 6
Outputs:
- transformed: float32 [2048, 1024], P('row', 'col')
The draws below stay inside these ranges and needn't reach their ends.
All inputs are finite; a program needn't handle non-finite values.
Results may differ from the reference program's by a relative error of at most 0.0003.
Values sent between devices are 32-bit elements; how exact they have to be, the bound alone decides.
A program may use at most 192 MiB of HBM per device.

```python
import jax
import jax.numpy as jnp
from jax import lax

REFL = 256
SWEEPS = 3
BLOCK_ROWS = 512
NBLOCKS = 8
NROWS = 2048
NCOLS = 1024


def steps_of(key, dims, shards, least, high):
    level, own = 1.0, jax.random.fold_in(key, 6)
    for dim, parts in shards:
        steps = jnp.exp(jax.random.uniform(jax.random.fold_in(own, dim), (parts,), jnp.float32, least / len(shards), high / len(shards)))
        level = level * jnp.repeat(steps, dims[dim] // parts).reshape([-1 if axis == dim else 1 for axis in range(len(dims))])
    return level


def scatter_about(stream_key, dims, deviation, bound, cuts=(), kind=jnp.bfloat16):
    result = jax.random.normal(stream_key, dims, jnp.float32) * deviation
    if len(cuts) > 0:
        result = steps_of(stream_key, dims, cuts, -0.22, 0.18) * result
    return jnp.clip(result, min=-bound, max=bound).astype(kind)


def setup_inputs(seed: int = 0) -> dict:
    keys = jax.random.split(jax.random.key(seed), 3)
    return {
        "eigenvectors": scatter_about(keys[0], (NROWS, NCOLS), 1.0, 6.0, ((0, 4), (1, 8)), jnp.float32),
        "householder": scatter_about(keys[1], (SWEEPS, NBLOCKS, BLOCK_ROWS, REFL), 1.0, 6.0, ((1, 4), (3, 8)), jnp.float32),
    }


PRECISE = lax.Precision.HIGHEST


def inner_product(left, right):
    return lax.dot_general(left, right, (((0,), (0,)), ((), ())), precision=PRECISE, preferred_element_type=jnp.float32)


def product(left, right):
    return jnp.dot(left, right, precision=PRECISE, preferred_element_type=jnp.float32)


def invert_upper(upper):
    order = upper.shape[0]
    rows_idx = lax.broadcasted_iota(jnp.int32, (order, order), 0)
    cols_idx = lax.broadcasted_iota(jnp.int32, (order, order), 1)
    inverse = jnp.where(rows_idx == cols_idx, 1.0 / jnp.diagonal(upper)[:, None], jnp.float32(0.0))
    size = 1
    while size < order:
        inside_old = (rows_idx // size) == (cols_idx // size)
        inside_new = (rows_idx // (2 * size)) == (cols_idx // (2 * size))
        corners = jnp.where(inside_new & jnp.logical_not(inside_old), upper, jnp.float32(0.0))
        inverse = inverse - product(product(inverse, corners), inverse)
        size = 2 * size
    return inverse


def reflect(stripe, vectors):
    gram_matrix = inner_product(vectors, vectors)
    upper_part = jnp.triu(gram_matrix, 1) + jnp.diag(jnp.diagonal(gram_matrix) * 0.5)
    weights = inner_product(vectors, stripe)
    scaled = product(invert_upper(upper_part), weights)
    return stripe - product(vectors, scaled)


def reference(eigenvectors, householder):
    matrix = eigenvectors
    for sweep_index in range(SWEEPS):
        sweep_vectors = householder[sweep_index]

        def apply_block(block_index, current):
            vectors = lax.dynamic_index_in_dim(sweep_vectors, block_index, 0, False)
            first_row = ((block_index - 1) * REFL).astype(jnp.int32)
            stripe = lax.dynamic_slice_in_dim(current, first_row, 2 * REFL, 0)
            return lax.dynamic_update_slice_in_dim(current, reflect(stripe, vectors), first_row, 0)

        matrix = lax.fori_loop(1, NBLOCKS, apply_block, matrix)
    return matrix
```

```python
import functools
import jax
import jax.numpy as jnp
from jax import lax
from jax.experimental import pallas as pl
from jax.experimental.pallas import tpu as pltpu
from jax.sharding import PartitionSpec as P

MESH = pl.DeviceIdType.MESH
F32, BF16 = jnp.float32, jnp.bfloat16


def dot(a, b):
    return jnp.dot(a, b, preferred_element_type=F32)


def dot_nt(a, b):
    return lax.dot_general(a, b, (((1,), (1,)), ((), ())), preferred_element_type=F32)


def split(x):
    high = x.astype(BF16)
    return high, (x - high.astype(F32)).astype(BF16)


def left_pair(x):
    return jnp.concatenate(split(x), axis=1)


def right_pair(x):
    row = jnp.concatenate(split(x), axis=1)
    return jnp.concatenate([row, row], axis=0)


def fold(left, right):
    both = dot(left, right)
    half = both.shape[1] // 2
    return both[:, :half] + both[:, half:]


def kernel(outer, inner, rows_n, y_ref, vt_ref, o_ref, vt_all, qh, ql, mid, low, tx_up, tx_dn,
           rx_dn, rx_up, oa_send, oa_recv, ib_send, ib_recv, up_send, up_recv, dn_send, dn_recv):
    sweeps, per, share, block = vt_ref.shape
    refl = share * outer * inner
    half = refl // 2
    d = lax.axis_index("row")
    c = lax.axis_index("col")
    zc, yc = lax.div(c, inner), lax.rem(c, inner)

    def z_at(step):
        return lax.rem(zc + step, outer)

    def y_at(step):
        return lax.rem(yc + step, inner)

    def place(s, j, z, y):
        start = pl.multiple_of((z * inner + y) * share, share)
        return vt_all.at[s, j, pl.ds(start, share)]

    barrier = pltpu.get_barrier_semaphore()
    for step in range(1, outer):
        pl.semaphore_signal(barrier, inc=1, device_id={"col": z_at(step) * inner + yc}, device_id_type=MESH)
    for step in range(1, inner):
        pl.semaphore_signal(barrier, inc=1, device_id={"col": zc * inner + y_at(step)}, device_id_type=MESH)

    @pl.when(d > 0)
    def _():
        pl.semaphore_signal(barrier, inc=1, device_id={"row": d - 1}, device_id_type=MESH)

    @pl.when(d < rows_n - 1)
    def _():
        pl.semaphore_signal(barrier, inc=1, device_id={"row": d + 1}, device_id_type=MESH)

    greeted = (outer - 1) + (inner - 1)
    pl.semaphore_wait(barrier, greeted + jnp.where(d > 0, 1, 0) + jnp.where(d < rows_n - 1, 1, 0))

    def used(j):
        return jnp.logical_or(d > 0, j > 0)

    def outer_copy(s, j, step):
        return pltpu.make_async_remote_copy(
            src_ref=vt_ref.at[s, j], dst_ref=place(s, j, zc, yc),
            send_sem=oa_send.at[s, j, step - 1], recv_sem=oa_recv.at[s, j, zc],
            device_id={"col": z_at(step) * inner + yc}, device_id_type=MESH)

    def outer_arrival(s, j, step):
        z = z_at(step)
        return pltpu.make_async_remote_copy(
            src_ref=vt_ref.at[s, j], dst_ref=place(s, j, z, yc),
            send_sem=oa_send.at[s, j, step - 1], recv_sem=oa_recv.at[s, j, z],
            device_id={"col": z * inner + yc}, device_id_type=MESH)

    def inner_copy(s, j, step, hop):
        z = z_at(step)
        source = vt_ref.at[s, j] if step == 0 else place(s, j, z, yc)
        return pltpu.make_async_remote_copy(
            src_ref=source, dst_ref=place(s, j, z, yc),
            send_sem=ib_send.at[s, j, step, hop - 1], recv_sem=ib_recv.at[s, j, z, yc],
            device_id={"col": zc * inner + y_at(hop)}, device_id_type=MESH)

    def inner_arrival(s, j, step, hop):
        z, y = z_at(step), y_at(hop)
        return pltpu.make_async_remote_copy(
            src_ref=vt_ref.at[s, j], dst_ref=place(s, j, z, y),
            send_sem=ib_send.at[s, j, step, hop - 1], recv_sem=ib_recv.at[s, j, z, y],
            device_id={"col": zc * inner + y}, device_id_type=MESH)

    def up_copy(s):
        return pltpu.make_async_remote_copy(
            src_ref=tx_up.at[s], dst_ref=rx_up.at[s], send_sem=up_send.at[s], recv_sem=up_recv.at[s],
            device_id={"row": lax.max(d - 1, 0)}, device_id_type=MESH)

    def dn_copy(s):
        return pltpu.make_async_remote_copy(
            src_ref=tx_dn.at[s], dst_ref=rx_dn.at[s], send_sem=dn_send.at[s], recv_sem=dn_recv.at[s],
            device_id={"row": lax.min(d + 1, rows_n - 1)}, device_id_type=MESH)

    def own_inner(s):
        for j in range(per):
            @pl.when(used(j))
            def _():
                for hop in range(1, inner):
                    inner_copy(s, j, 0, hop).start()

    def forward(s, j, step, more=True):
        @pl.when(jnp.logical_and(used(j), more))
        def _():
            outer_arrival(s, j, step).wait_recv()
            for hop in range(1, inner):
                inner_copy(s, j, step, hop).start()

    for s in range(sweeps):
        for j in range(per):
            @pl.when(used(j))
            def _():
                for step in range(1, outer):
                    outer_copy(s, j, step).start()
        if s < 2:
            own_inner(s)

    for s in range(sweeps):
        for j in range(per):
            place(s, j, zc, yc)[...] = vt_ref[s, j]
    mid[...] = y_ref[:refl]
    low[...] = y_ref[refl:]

    for step in range(1, outer):
        for j in range(per):
            forward(0, j, step)

    rows_i = lax.broadcasted_iota(jnp.int32, (half, half), 0)
    cols_i = lax.broadcasted_iota(jnp.int32, (half, half), 1)
    on_diagonal = rows_i == cols_i
    above = rows_i < cols_i

    def prepare(s, points):
        points = list(points)

        def point():
            if points:
                points.pop(0)()

        vs, chains, corners = [], [], []
        for j in range(per):
            slot = jnp.where(d > 0, j, per - 1) if j == 0 else j
            vt = vt_all[s, slot]
            vh, vl = split(vt)
            vs.append((slot, vh, vl))
            top = dot_nt(vh[:half], vh) + dot_nt(vh[:half], vl) + dot_nt(vl[:half], vh)
            end = dot_nt(vh[half:], vh[half:]) + dot_nt(vh[half:], vl[half:]) + dot_nt(vl[half:], vh[half:])
            corners.append(top[:, half:])
            for gram in (top[:, :half], end):
                on = jnp.where(on_diagonal, gram, 0.0) * 0.5
                by_row = 1.0 / jnp.sum(on, axis=1, keepdims=True)
                by_col = 1.0 / jnp.sum(on, axis=0, keepdims=True)
                pairs = jnp.where(above & (rows_i // 2 == cols_i // 2), gram, 0.0)
                inverse = jnp.where(on_diagonal, by_row, 0.0) - by_row * pairs * by_col
                chains.append((gram, inverse))
        point()
        size = 2
        while size < half:
            joined = above & (rows_i // (2 * size) == cols_i // (2 * size)) & (rows_i // size != cols_i // size)
            first = [fold(left_pair(inv), right_pair(jnp.where(joined, gram, 0.0))) for gram, inv in chains]
            chains = [(gram, inv - fold(left_pair(f), right_pair(inv))) for (gram, inv), f in zip(chains, first)]
            size *= 2
            point()
        for j in range(per):
            slot, vh, vl = vs[j]
            p1, p2 = chains[2 * j][1], chains[2 * j + 1][1]
            corner = -fold(left_pair(fold(left_pair(p1), right_pair(corners[j]))), right_pair(p2))
            v = vt_all[s, slot].T
            v1, v2 = left_pair(v[:, :half]), left_pair(v[:, half:])
            a = jnp.concatenate(
                [fold(v1, right_pair(p1)), fold(v1, right_pair(corner)) + fold(v2, right_pair(p2))], axis=1)
            ah, al = split(a)
            for base in range(0, block, refl):
                ahb, alb = ah[base:base + refl], al[base:base + refl]
                q_rows = lax.broadcasted_iota(jnp.int32, (refl, block), 0) + base
                q_cols = lax.broadcasted_iota(jnp.int32, (refl, block), 1)
                unit = jnp.where(q_rows == q_cols, 1.0, 0.0)
                q = unit - (dot(ahb, vh) + dot(ahb, vl) + dot(alb, vh))
                hi, lo = split(q)
                qh[j, base:base + refl] = hi
                ql[j, base:base + refl] = lo
        while points:
            point()

    def apply_half(j, base, y_pair, y_high):
        both = dot(qh[j, base:base + refl], y_pair)
        cols = y_high.shape[1]
        return both[:, :cols] + both[:, cols:] + dot(ql[j, base:base + refl], y_high)

    def sweep(s, carry):
        nxt = lax.min(s + 1, sweeps - 1)
        more = s + 1 < sweeps

        @pl.when(s + 2 < sweeps)
        def _():
            own_inner(lax.min(s + 2, sweeps - 1))

        for j in range(per):
            @pl.when(used(j))
            def _():
                for step in range(outer):
                    for hop in range(1, inner):
                        inner_arrival(s, j, step, hop).wait_recv()

        prepare(s, [functools.partial(forward, nxt, j, step, more) for step in range(1, outer) for j in range(per)])

        @pl.when(d > 0)
        def _():
            dn_copy(s).wait_recv()
            y = jnp.concatenate([rx_dn[s], mid[...]], axis=0)
            high, rest = split(y)
            y_pair = jnp.concatenate([high, rest], axis=1)
            tx_up[s] = apply_half(0, 0, y_pair, high)
            up_copy(s).start()
            mid[...] = apply_half(0, refl, y_pair, high)

        @pl.when(jnp.logical_and(d < rows_n - 1, s > 0))
        def _():
            before = lax.max(s - 1, 0)
            up_copy(before).wait_recv()
            low[...] = rx_up[before]

        y = jnp.concatenate([mid[...], low[...]], axis=0)
        high, rest = split(y)
        y_pair = jnp.concatenate([high, rest], axis=1)
        new_low = apply_half(1, refl, y_pair, high)
        low[...] = new_low
        tx_dn[s] = new_low

        @pl.when(d < rows_n - 1)
        def _():
            dn_copy(s).start()

        mid[...] = apply_half(1, 0, y_pair, high)
        return carry

    lax.fori_loop(0, sweeps, sweep, 0)

    o_ref[:refl] = mid[...]

    @pl.when(d < rows_n - 1)
    def _():
        up_copy(sweeps - 1).wait_recv()
        o_ref[refl:] = rx_up[sweeps - 1]

    @pl.when(d == rows_n - 1)
    def _():
        o_ref[refl:] = low[...]

    for s in range(sweeps):
        for j in range(per):
            @pl.when(used(j))
            def _():
                for step in range(1, outer):
                    outer_copy(s, j, step).wait_send()
                for step in range(outer):
                    for hop in range(1, inner):
                        inner_copy(s, j, step, hop).wait_send()

        @pl.when(d > 0)
        def _():
            up_copy(s).wait_send()

        @pl.when(d < rows_n - 1)
        def _():
            dn_copy(s).wait_send()


def solution(mesh):
    rows_n, cols_n = mesh.shape["row"], mesh.shape["col"]
    inner = 1
    while (2 * inner) * (2 * inner) <= cols_n and cols_n % (2 * inner) == 0:
        inner *= 2
    outer = cols_n // inner

    def shards(eigenvectors, householder):
        vt = jnp.swapaxes(householder, 2, 3)
        sweeps, per, share, block = vt.shape
        rows, cols = eigenvectors.shape
        refl = share * cols_n
        dma = pltpu.SemaphoreType.DMA
        vmem = pl.BlockSpec(memory_space=pltpu.VMEM)
        return pl.pallas_call(
            functools.partial(kernel, outer, inner, rows_n),
            out_shape=jax.ShapeDtypeStruct((rows, cols), F32),
            in_specs=[vmem] * 2,
            out_specs=vmem,
            scratch_shapes=[
                pltpu.VMEM((sweeps, per, refl, block), F32),
                pltpu.VMEM((per, block, block), BF16),
                pltpu.VMEM((per, block, block), BF16),
                pltpu.VMEM((refl, cols), F32),
                pltpu.VMEM((refl, cols), F32),
                pltpu.VMEM((sweeps, refl, cols), F32),
                pltpu.VMEM((sweeps, refl, cols), F32),
                pltpu.VMEM((sweeps, refl, cols), F32),
                pltpu.VMEM((sweeps, refl, cols), F32),
                dma((sweeps, per, outer)),
                dma((sweeps, per, outer)),
                dma((sweeps, per, outer, inner)),
                dma((sweeps, per, outer, inner)),
                dma((sweeps,)), dma((sweeps,)), dma((sweeps,)), dma((sweeps,)),
            ],
            compiler_params=pltpu.CompilerParams(
                collective_id=0, has_side_effects=True, vmem_limit_bytes=60 * 2**20),
        )(eigenvectors, vt)

    return jax.shard_map(
        shards, mesh=mesh, in_specs=(P("row", "col"), P(None, "row", None, "col")),
        out_specs=P("row", "col"), check_vma=False)
```

```python
import functools
import jax
import jax.numpy as jnp
from jax import lax
from jax.experimental import pallas as pl
from jax.experimental.pallas import tpu as pltpu
from jax.sharding import PartitionSpec as P

MESH = pl.DeviceIdType.MESH
F32, BF16 = jnp.float32, jnp.bfloat16


def dot(a, b):
    return jnp.dot(a, b, preferred_element_type=F32)


def dot_nt(a, b):
    return lax.dot_general(a, b, (((1,), (1,)), ((), ())), preferred_element_type=F32)


def split(x):
    high = x.astype(BF16)
    return high, (x - high.astype(F32)).astype(BF16)


def left_pair(x):
    return jnp.concatenate(split(x), axis=1)


def right_pair(x):
    row = jnp.concatenate(split(x), axis=1)
    return jnp.concatenate([row, row], axis=0)


def fold(left, right):
    both = dot(left, right)
    half = both.shape[1] // 2
    return both[:, :half] + both[:, half:]


def kernel(outer, inner, rows_n, y_ref, vt_ref, o_ref, vt_all, qh, ql, mid, low, tx_up, tx_dn,
           rx_dn, rx_up, oa_send, oa_recv, ib_send, ib_recv, up_send, up_recv, dn_send, dn_recv):
    sweeps, per, share, block = vt_ref.shape
    refl = share * outer * inner
    half = refl // 2
    d = lax.axis_index("row")
    c = lax.axis_index("col")
    zc, yc = lax.div(c, inner), lax.rem(c, inner)

    def z_at(step):
        return lax.rem(zc + step, outer)

    def y_at(step):
        return lax.rem(yc + step, inner)

    def place(s, j, z, y):
        start = pl.multiple_of((z * inner + y) * share, share)
        return vt_all.at[s, j, pl.ds(start, share)]

    barrier = pltpu.get_barrier_semaphore()
    for step in range(1, outer):
        pl.semaphore_signal(barrier, inc=1, device_id={"col": z_at(step) * inner + yc}, device_id_type=MESH)
    for step in range(1, inner):
        pl.semaphore_signal(barrier, inc=1, device_id={"col": zc * inner + y_at(step)}, device_id_type=MESH)

    @pl.when(d > 0)
    def _():
        pl.semaphore_signal(barrier, inc=1, device_id={"row": d - 1}, device_id_type=MESH)

    @pl.when(d < rows_n - 1)
    def _():
        pl.semaphore_signal(barrier, inc=1, device_id={"row": d + 1}, device_id_type=MESH)

    greeted = (outer - 1) + (inner - 1)
    pl.semaphore_wait(barrier, greeted + jnp.where(d > 0, 1, 0) + jnp.where(d < rows_n - 1, 1, 0))

    def used(j):
        return jnp.logical_or(d > 0, j > 0)

    def outer_copy(s, j, z, side, own=False):
        there = lax.min(zc + 1, outer - 1) if side == 0 else lax.max(zc - 1, 0)
        return pltpu.make_async_remote_copy(
            src_ref=vt_ref.at[s, j] if own else place(s, j, z, yc), dst_ref=place(s, j, z, yc),
            send_sem=oa_send.at[s, j, side, z], recv_sem=oa_recv.at[s, j, z],
            device_id={"col": there * inner + yc}, device_id_type=MESH)

    def goes_on(side):
        return zc < outer - 1 if side == 0 else zc > 0

    def piece_at(side, distance):
        if side == 0:
            return lax.max(zc - distance, 0), zc - distance >= 0
        return lax.min(zc + distance, outer - 1), zc + distance < outer

    def inner_copy(s, j, z, hop, own=False):
        return pltpu.make_async_remote_copy(
            src_ref=vt_ref.at[s, j] if own else place(s, j, z, yc), dst_ref=place(s, j, z, yc),
            send_sem=ib_send.at[s, j, z, hop - 1], recv_sem=ib_recv.at[s, j, z, yc],
            device_id={"col": zc * inner + y_at(hop)}, device_id_type=MESH)

    def inner_arrival(s, j, z, hop):
        y = y_at(hop)
        return pltpu.make_async_remote_copy(
            src_ref=vt_ref.at[s, j], dst_ref=place(s, j, z, y),
            send_sem=ib_send.at[s, j, z, hop - 1], recv_sem=ib_recv.at[s, j, z, y],
            device_id={"col": zc * inner + y}, device_id_type=MESH)

    def up_copy(s):
        return pltpu.make_async_remote_copy(
            src_ref=tx_up.at[s], dst_ref=rx_up.at[s], send_sem=up_send.at[s], recv_sem=up_recv.at[s],
            device_id={"row": lax.max(d - 1, 0)}, device_id_type=MESH)

    def dn_copy(s):
        return pltpu.make_async_remote_copy(
            src_ref=tx_dn.at[s], dst_ref=rx_dn.at[s], send_sem=dn_send.at[s], recv_sem=dn_recv.at[s],
            device_id={"row": lax.min(d + 1, rows_n - 1)}, device_id_type=MESH)

    def own_inner(s):
        for j in range(per):
            @pl.when(used(j))
            def _():
                for hop in range(1, inner):
                    inner_copy(s, j, zc, hop, True).start()

    def forward(s, j, distance, more=True):
        for side in (0, 1):
            z, there = piece_at(side, distance)

            @pl.when(jnp.logical_and(jnp.logical_and(used(j), there), more))
            def _():
                outer_copy(s, j, z, side).wait_recv()

                @pl.when(goes_on(side))
                def _():
                    outer_copy(s, j, z, side).start()

                for hop in range(1, inner):
                    inner_copy(s, j, z, hop).start()

    for s in range(sweeps):
        for j in range(per):
            for side in (0, 1):
                @pl.when(jnp.logical_and(used(j), goes_on(side)))
                def _():
                    outer_copy(s, j, zc, side, True).start()
        if s < 2:
            own_inner(s)

    for s in range(sweeps):
        for j in range(per):
            place(s, j, zc, yc)[...] = vt_ref[s, j]
    mid[...] = y_ref[:refl]
    low[...] = y_ref[refl:]

    pieces = [(j, distance) for j in range(per) for distance in range(1, outer)]
    ahead = min(2, len(pieces))
    for j, step in pieces:
        forward(0, j, step)
    if sweeps > 1:
        for j, step in pieces[:ahead]:
            forward(1, j, step)

    rows_i = lax.broadcasted_iota(jnp.int32, (half, half), 0)
    cols_i = lax.broadcasted_iota(jnp.int32, (half, half), 1)
    on_diagonal = rows_i == cols_i
    above = rows_i < cols_i

    def prepare(s, points):
        points = list(points)

        def point():
            if points:
                points.pop(0)()

        vs, chains, corners = [], [], []
        for j in range(per):
            slot = jnp.where(d > 0, j, per - 1) if j == 0 else j
            vt = vt_all[s, slot]
            vh, vl = split(vt)
            vs.append((slot, vh, vl))
            top = dot_nt(vh[:half], vh) + dot_nt(vh[:half], vl) + dot_nt(vl[:half], vh)
            end = dot_nt(vh[half:], vh[half:]) + dot_nt(vh[half:], vl[half:]) + dot_nt(vl[half:], vh[half:])
            corners.append(top[:, half:])
            for gram in (top[:, :half], end):
                on = jnp.where(on_diagonal, gram, 0.0) * 0.5
                by_row = 1.0 / jnp.sum(on, axis=1, keepdims=True)
                by_col = 1.0 / jnp.sum(on, axis=0, keepdims=True)
                pairs = jnp.where(above & (rows_i // 2 == cols_i // 2), gram, 0.0)
                inverse = jnp.where(on_diagonal, by_row, 0.0) - by_row * pairs * by_col
                chains.append((gram, inverse))
        point()
        size = 2
        while size < half:
            joined = above & (rows_i // (2 * size) == cols_i // (2 * size)) & (rows_i // size != cols_i // size)
            first = [fold(left_pair(inv), right_pair(jnp.where(joined, gram, 0.0))) for gram, inv in chains]
            chains = [(gram, inv - fold(left_pair(f), right_pair(inv))) for (gram, inv), f in zip(chains, first)]
            size *= 2
            point()
        for j in range(per):
            slot, vh, vl = vs[j]
            p1, p2 = chains[2 * j][1], chains[2 * j + 1][1]
            corner = -fold(left_pair(fold(left_pair(p1), right_pair(corners[j]))), right_pair(p2))
            v = vt_all[s, slot].T
            v1, v2 = left_pair(v[:, :half]), left_pair(v[:, half:])
            a = jnp.concatenate(
                [fold(v1, right_pair(p1)), fold(v1, right_pair(corner)) + fold(v2, right_pair(p2))], axis=1)
            ah, al = split(a)
            for base in range(0, block, refl):
                ahb, alb = ah[base:base + refl], al[base:base + refl]
                q_rows = lax.broadcasted_iota(jnp.int32, (refl, block), 0) + base
                q_cols = lax.broadcasted_iota(jnp.int32, (refl, block), 1)
                unit = jnp.where(q_rows == q_cols, 1.0, 0.0)
                q = unit - (dot(ahb, vh) + dot(ahb, vl) + dot(alb, vh))
                hi, lo = split(q)
                qh[j, base:base + refl] = hi
                ql[j, base:base + refl] = lo
        while points:
            point()

    def apply_half(j, base, y_pair, y_high):
        both = dot(qh[j, base:base + refl], y_pair)
        cols = y_high.shape[1]
        return both[:, :cols] + both[:, cols:] + dot(ql[j, base:base + refl], y_high)

    def sweep(s, carry):
        nxt, later = lax.min(s + 1, sweeps - 1), lax.min(s + 2, sweeps - 1)
        more, still = s + 1 < sweeps, s + 2 < sweeps

        @pl.when(still)
        def _():
            own_inner(later)

        for j in range(per):
            @pl.when(used(j))
            def _():
                for z in range(outer):
                    for hop in range(1, inner):
                        inner_arrival(s, j, z, hop).wait_recv()

        def early(i):
            return 2 * d >= i

        points = []
        for i, (j, step) in list(enumerate(pieces))[ahead:]:
            waits = jnp.logical_and(more, jnp.logical_not(jnp.logical_and(s > 0, early(i))))
            points.append(functools.partial(forward, nxt, j, step, waits))
        points += [functools.partial(forward, later, j, step, still) for j, step in pieces[:ahead]]
        prepare(s, points)
        for i, (j, step) in list(enumerate(pieces))[ahead:]:
            forward(later, j, step, jnp.logical_and(still, early(i)))

        @pl.when(d > 0)
        def _():
            dn_copy(s).wait_recv()
            y = jnp.concatenate([rx_dn[s], mid[...]], axis=0)
            high, rest = split(y)
            y_pair = jnp.concatenate([high, rest], axis=1)
            tx_up[s] = apply_half(0, 0, y_pair, high)
            up_copy(s).start()
            mid[...] = apply_half(0, refl, y_pair, high)

        @pl.when(jnp.logical_and(d < rows_n - 1, s > 0))
        def _():
            before = lax.max(s - 1, 0)
            up_copy(before).wait_recv()
            low[...] = rx_up[before]

        y = jnp.concatenate([mid[...], low[...]], axis=0)
        high, rest = split(y)
        y_pair = jnp.concatenate([high, rest], axis=1)
        new_low = apply_half(1, refl, y_pair, high)
        low[...] = new_low
        tx_dn[s] = new_low

        @pl.when(d < rows_n - 1)
        def _():
            dn_copy(s).start()

        mid[...] = apply_half(1, 0, y_pair, high)
        return carry

    lax.fori_loop(0, sweeps, sweep, 0)

    o_ref[:refl] = mid[...]

    @pl.when(d < rows_n - 1)
    def _():
        up_copy(sweeps - 1).wait_recv()
        o_ref[refl:] = rx_up[sweeps - 1]

    @pl.when(d == rows_n - 1)
    def _():
        o_ref[refl:] = low[...]

    for s in range(sweeps):
        for j in range(per):
            @pl.when(used(j))
            def _():
                for z in range(outer):
                    for hop in range(1, inner):
                        inner_copy(s, j, z, hop).wait_send()
                for side in (0, 1):
                    for distance in range(outer):
                        z, there = piece_at(side, distance)

                        @pl.when(jnp.logical_and(there, goes_on(side)))
                        def _():
                            outer_copy(s, j, z, side).wait_send()

        @pl.when(d > 0)
        def _():
            up_copy(s).wait_send()

        @pl.when(d < rows_n - 1)
        def _():
            dn_copy(s).wait_send()


def solution(mesh):
    rows_n, cols_n = mesh.shape["row"], mesh.shape["col"]
    inner = 1
    while (2 * inner) * (2 * inner) <= cols_n and cols_n % (2 * inner) == 0:
        inner *= 2
    outer = cols_n // inner

    def shards(eigenvectors, householder):
        vt = jnp.swapaxes(householder, 2, 3)
        sweeps, per, share, block = vt.shape
        rows, cols = eigenvectors.shape
        refl = share * cols_n
        dma = pltpu.SemaphoreType.DMA
        vmem = pl.BlockSpec(memory_space=pltpu.VMEM)
        return pl.pallas_call(
            functools.partial(kernel, outer, inner, rows_n),
            out_shape=jax.ShapeDtypeStruct((rows, cols), F32),
            in_specs=[vmem] * 2,
            out_specs=vmem,
            scratch_shapes=[
                pltpu.VMEM((sweeps, per, refl, block), F32),
                pltpu.VMEM((per, block, block), BF16),
                pltpu.VMEM((per, block, block), BF16),
                pltpu.VMEM((refl, cols), F32),
                pltpu.VMEM((refl, cols), F32),
                pltpu.VMEM((sweeps, refl, cols), F32),
                pltpu.VMEM((sweeps, refl, cols), F32),
                pltpu.VMEM((sweeps, refl, cols), F32),
                pltpu.VMEM((sweeps, refl, cols), F32),
                dma((sweeps, per, 2, outer)),
                dma((sweeps, per, outer)),
                dma((sweeps, per, outer, inner)),
                dma((sweeps, per, outer, inner)),
                dma((sweeps,)), dma((sweeps,)), dma((sweeps,)), dma((sweeps,)),
            ],
            compiler_params=pltpu.CompilerParams(
                collective_id=0, has_side_effects=True, vmem_limit_bytes=60 * 2**20),
        )(eigenvectors, vt)

    return jax.shard_map(
        shards, mesh=mesh, in_specs=(P("row", "col"), P(None, "row", None, "col")),
        out_specs=P("row", "col"), check_vma=False)
```

```python
import functools
import jax
import jax.numpy as jnp
from jax import lax
from jax.experimental import pallas as pl
from jax.experimental.pallas import tpu as pltpu
from jax.sharding import PartitionSpec as P

MESH = pl.DeviceIdType.MESH
F32, BF16 = jnp.float32, jnp.bfloat16


def dot(a, b):
    return jnp.dot(a, b, preferred_element_type=F32)


def dot_nt(a, b):
    return lax.dot_general(a, b, (((1,), (1,)), ((), ())), preferred_element_type=F32)


def split(x):
    high = x.astype(BF16)
    return high, (x - high.astype(F32)).astype(BF16)


def left_pair(x):
    return jnp.concatenate(split(x), axis=1)


def right_pair(x):
    row = jnp.concatenate(split(x), axis=1)
    return jnp.concatenate([row, row], axis=0)


def fold(left, right):
    both = dot(left, right)
    half = both.shape[1] // 2
    return both[:, :half] + both[:, half:]


def kernel(outer, inner, rows_n, y_ref, vt_ref, o_ref, vt_all, qh, ql, mid, low, tx_up, tx_dn,
           rx_dn, rx_up, oa_send, oa_recv, ib_send, ib_recv, up_send, up_recv, dn_send, dn_recv):
    sweeps, per, share, block = vt_ref.shape
    refl = share * outer * inner
    half = refl // 2
    d = lax.axis_index("row")
    c = lax.axis_index("col")
    zc, yc = lax.div(c, inner), lax.rem(c, inner)

    def z_at(step):
        return lax.rem(zc + step, outer)

    def y_at(step):
        return lax.rem(yc + step, inner)

    def place(s, j, z, y):
        start = pl.multiple_of((z * inner + y) * share, share)
        return vt_all.at[s, j, pl.ds(start, share)]

    barrier = pltpu.get_barrier_semaphore()
    for step in range(1, outer):
        pl.semaphore_signal(barrier, inc=1, device_id={"col": z_at(step) * inner + yc}, device_id_type=MESH)
    for step in range(1, inner):
        pl.semaphore_signal(barrier, inc=1, device_id={"col": zc * inner + y_at(step)}, device_id_type=MESH)

    @pl.when(d > 0)
    def _():
        pl.semaphore_signal(barrier, inc=1, device_id={"row": d - 1}, device_id_type=MESH)

    @pl.when(d < rows_n - 1)
    def _():
        pl.semaphore_signal(barrier, inc=1, device_id={"row": d + 1}, device_id_type=MESH)

    greeted = (outer - 1) + (inner - 1)
    pl.semaphore_wait(barrier, greeted + jnp.where(d > 0, 1, 0) + jnp.where(d < rows_n - 1, 1, 0))

    def used(j):
        return jnp.logical_or(d > 0, j > 0)

    def outer_copy(s, j, z, side, own=False):
        there = lax.min(zc + 1, outer - 1) if side == 0 else lax.max(zc - 1, 0)
        return pltpu.make_async_remote_copy(
            src_ref=vt_ref.at[s, j] if own else place(s, j, z, yc), dst_ref=place(s, j, z, yc),
            send_sem=oa_send.at[s, j, side, z], recv_sem=oa_recv.at[s, j, z],
            device_id={"col": there * inner + yc}, device_id_type=MESH)

    def goes_on(side):
        return zc < outer - 1 if side == 0 else zc > 0

    def piece_at(side, distance):
        if side == 0:
            return lax.max(zc - distance, 0), zc - distance >= 0
        return lax.min(zc + distance, outer - 1), zc + distance < outer

    def inner_copy(s, j, z, hop, own=False):
        return pltpu.make_async_remote_copy(
            src_ref=vt_ref.at[s, j] if own else place(s, j, z, yc), dst_ref=place(s, j, z, yc),
            send_sem=ib_send.at[s, j, z, hop - 1], recv_sem=ib_recv.at[s, j, z, yc],
            device_id={"col": zc * inner + y_at(hop)}, device_id_type=MESH)

    def inner_arrival(s, j, z, hop):
        y = y_at(hop)
        return pltpu.make_async_remote_copy(
            src_ref=vt_ref.at[s, j], dst_ref=place(s, j, z, y),
            send_sem=ib_send.at[s, j, z, hop - 1], recv_sem=ib_recv.at[s, j, z, y],
            device_id={"col": zc * inner + y}, device_id_type=MESH)

    def up_copy(s):
        return pltpu.make_async_remote_copy(
            src_ref=tx_up.at[s], dst_ref=rx_up.at[s], send_sem=up_send.at[s], recv_sem=up_recv.at[s],
            device_id={"row": lax.max(d - 1, 0)}, device_id_type=MESH)

    def dn_copy(s):
        return pltpu.make_async_remote_copy(
            src_ref=tx_dn.at[s], dst_ref=rx_dn.at[s], send_sem=dn_send.at[s], recv_sem=dn_recv.at[s],
            device_id={"row": lax.min(d + 1, rows_n - 1)}, device_id_type=MESH)

    def own_inner(s):
        for j in range(per):
            @pl.when(used(j))
            def _():
                for hop in range(1, inner):
                    inner_copy(s, j, zc, hop, True).start()

    def forward(s, j, distance, more=True):
        for side in (0, 1):
            z, there = piece_at(side, distance)

            @pl.when(jnp.logical_and(jnp.logical_and(used(j), there), more))
            def _():
                outer_copy(s, j, z, side).wait_recv()

                @pl.when(goes_on(side))
                def _():
                    outer_copy(s, j, z, side).start()

                for hop in range(1, inner):
                    inner_copy(s, j, z, hop).start()

    def own_outer(s):
        for j in range(per):
            for side in (0, 1):
                @pl.when(jnp.logical_and(used(j), goes_on(side)))
                def _():
                    outer_copy(s, j, zc, side, True).start()

    for s in range(min(sweeps, 2)):
        own_outer(s)
        own_inner(s)

    for s in range(sweeps):
        for j in range(per):
            place(s, j, zc, yc)[...] = vt_ref[s, j]
    mid[...] = y_ref[:refl]
    low[...] = y_ref[refl:]

    pieces = [(j, distance) for j in range(per) for distance in range(1, outer)]
    ahead = min(2, len(pieces))
    for j, step in pieces:
        forward(0, j, step)
    if sweeps > 1:
        for j, step in pieces[:ahead]:
            forward(1, j, step)

    rows_i = lax.broadcasted_iota(jnp.int32, (half, half), 0)
    cols_i = lax.broadcasted_iota(jnp.int32, (half, half), 1)
    on_diagonal = rows_i == cols_i
    above = rows_i < cols_i

    def prepare(s, points):
        points = list(points)

        def point():
            if points:
                points.pop(0)()

        vs, chains, corners = [], [], []
        for j in range(per):
            slot = jnp.where(d > 0, j, per - 1) if j == 0 else j
            vt = vt_all[s, slot]
            vh, vl = split(vt)
            vs.append((slot, vh, vl))
            top = dot_nt(vh[:half], vh) + dot_nt(vh[:half], vl) + dot_nt(vl[:half], vh)
            end = dot_nt(vh[half:], vh[half:]) + dot_nt(vh[half:], vl[half:]) + dot_nt(vl[half:], vh[half:])
            corners.append(top[:, half:])
            for gram in (top[:, :half], end):
                on = jnp.where(on_diagonal, gram, 0.0) * 0.5
                by_row = 1.0 / jnp.sum(on, axis=1, keepdims=True)
                by_col = 1.0 / jnp.sum(on, axis=0, keepdims=True)
                pairs = jnp.where(above & (rows_i // 2 == cols_i // 2), gram, 0.0)
                inverse = jnp.where(on_diagonal, by_row, 0.0) - by_row * pairs * by_col
                chains.append((gram, inverse))
        point()
        size = 2
        while size < half:
            joined = above & (rows_i // (2 * size) == cols_i // (2 * size)) & (rows_i // size != cols_i // size)
            first = [fold(left_pair(inv), right_pair(jnp.where(joined, gram, 0.0))) for gram, inv in chains]
            chains = [(gram, inv - fold(left_pair(f), right_pair(inv))) for (gram, inv), f in zip(chains, first)]
            size *= 2
            point()
        for j in range(per):
            slot, vh, vl = vs[j]
            p1, p2 = chains[2 * j][1], chains[2 * j + 1][1]
            corner = -fold(left_pair(fold(left_pair(p1), right_pair(corners[j]))), right_pair(p2))
            v = vt_all[s, slot].T
            v1, v2 = left_pair(v[:, :half]), left_pair(v[:, half:])
            a = jnp.concatenate(
                [fold(v1, right_pair(p1)), fold(v1, right_pair(corner)) + fold(v2, right_pair(p2))], axis=1)
            ah, al = split(a)
            for base in range(0, block, refl):
                ahb, alb = ah[base:base + refl], al[base:base + refl]
                q_rows = lax.broadcasted_iota(jnp.int32, (refl, block), 0) + base
                q_cols = lax.broadcasted_iota(jnp.int32, (refl, block), 1)
                unit = jnp.where(q_rows == q_cols, 1.0, 0.0)
                q = unit - (dot(ahb, vh) + dot(ahb, vl) + dot(alb, vh))
                hi, lo = split(q)
                qh[j, base:base + refl] = hi
                ql[j, base:base + refl] = lo
        while points:
            point()

    def apply_half(j, base, y_pair, y_high):
        both = dot(qh[j, base:base + refl], y_pair)
        cols = y_high.shape[1]
        return both[:, :cols] + both[:, cols:] + dot(ql[j, base:base + refl], y_high)

    def sweep(s, carry):
        nxt, later = lax.min(s + 1, sweeps - 1), lax.min(s + 2, sweeps - 1)
        more, still = s + 1 < sweeps, s + 2 < sweeps

        @pl.when(still)
        def _():
            own_outer(later)
            own_inner(later)

        for j in range(per):
            @pl.when(used(j))
            def _():
                for z in range(outer):
                    for hop in range(1, inner):
                        inner_arrival(s, j, z, hop).wait_recv()

        def early(i):
            return 2 * d >= i

        points = []
        for i, (j, step) in list(enumerate(pieces))[ahead:]:
            waits = jnp.logical_and(more, jnp.logical_not(jnp.logical_and(s > 0, early(i))))
            points.append(functools.partial(forward, nxt, j, step, waits))
        points += [functools.partial(forward, later, j, step, still) for j, step in pieces[:ahead]]
        prepare(s, points)
        for i, (j, step) in list(enumerate(pieces))[ahead:]:
            forward(later, j, step, jnp.logical_and(still, early(i)))

        @pl.when(d > 0)
        def _():
            dn_copy(s).wait_recv()
            y = jnp.concatenate([rx_dn[s], mid[...]], axis=0)
            high, rest = split(y)
            y_pair = jnp.concatenate([high, rest], axis=1)
            tx_up[s] = apply_half(0, 0, y_pair, high)
            up_copy(s).start()
            mid[...] = apply_half(0, refl, y_pair, high)

        @pl.when(jnp.logical_and(d < rows_n - 1, s > 0))
        def _():
            before = lax.max(s - 1, 0)
            up_copy(before).wait_recv()
            low[...] = rx_up[before]

        y = jnp.concatenate([mid[...], low[...]], axis=0)
        high, rest = split(y)
        y_pair = jnp.concatenate([high, rest], axis=1)
        new_low = apply_half(1, refl, y_pair, high)
        low[...] = new_low
        tx_dn[s] = new_low

        @pl.when(d < rows_n - 1)
        def _():
            dn_copy(s).start()

        mid[...] = apply_half(1, 0, y_pair, high)
        return carry

    lax.fori_loop(0, sweeps, sweep, 0)

    o_ref[:refl] = mid[...]

    @pl.when(d < rows_n - 1)
    def _():
        up_copy(sweeps - 1).wait_recv()
        o_ref[refl:] = rx_up[sweeps - 1]

    @pl.when(d == rows_n - 1)
    def _():
        o_ref[refl:] = low[...]

    for s in range(sweeps):
        for j in range(per):
            @pl.when(used(j))
            def _():
                for z in range(outer):
                    for hop in range(1, inner):
                        inner_copy(s, j, z, hop).wait_send()
                for side in (0, 1):
                    for distance in range(outer):
                        z, there = piece_at(side, distance)

                        @pl.when(jnp.logical_and(there, goes_on(side)))
                        def _():
                            outer_copy(s, j, z, side).wait_send()

        @pl.when(d > 0)
        def _():
            up_copy(s).wait_send()

        @pl.when(d < rows_n - 1)
        def _():
            dn_copy(s).wait_send()


def solution(mesh):
    rows_n, cols_n = mesh.shape["row"], mesh.shape["col"]
    inner = 1
    while (2 * inner) * (2 * inner) <= cols_n and cols_n % (2 * inner) == 0:
        inner *= 2
    outer = cols_n // inner

    def shards(eigenvectors, householder):
        vt = jnp.swapaxes(householder, 2, 3)
        sweeps, per, share, block = vt.shape
        rows, cols = eigenvectors.shape
        refl = share * cols_n
        dma = pltpu.SemaphoreType.DMA
        vmem = pl.BlockSpec(memory_space=pltpu.VMEM)
        return pl.pallas_call(
            functools.partial(kernel, outer, inner, rows_n),
            out_shape=jax.ShapeDtypeStruct((rows, cols), F32),
            in_specs=[vmem] * 2,
            out_specs=vmem,
            scratch_shapes=[
                pltpu.VMEM((sweeps, per, refl, block), F32),
                pltpu.VMEM((per, block, block), BF16),
                pltpu.VMEM((per, block, block), BF16),
                pltpu.VMEM((refl, cols), F32),
                pltpu.VMEM((refl, cols), F32),
                pltpu.VMEM((sweeps, refl, cols), F32),
                pltpu.VMEM((sweeps, refl, cols), F32),
                pltpu.VMEM((sweeps, refl, cols), F32),
                pltpu.VMEM((sweeps, refl, cols), F32),
                dma((sweeps, per, 2, outer)),
                dma((sweeps, per, outer)),
                dma((sweeps, per, outer, inner)),
                dma((sweeps, per, outer, inner)),
                dma((sweeps,)), dma((sweeps,)), dma((sweeps,)), dma((sweeps,)),
            ],
            compiler_params=pltpu.CompilerParams(
                collective_id=0, has_side_effects=True, vmem_limit_bytes=60 * 2**20),
        )(eigenvectors, vt)

    return jax.shard_map(
        shards, mesh=mesh, in_specs=(P("row", "col"), P(None, "row", None, "col")),
        out_specs=P("row", "col"), check_vma=False)
```
